32 devices in a mesh: dp: 8 (over z, core), expert: 4 (over y, x).
Axes of the slice: x: 2, y: 2, z: 4, core: 2. Of those that a mesh axis runs over, the one named last changes fastest.
Arguments:
- images: bfloat16 [128, 196, 768], P(('dp', 'expert')), may hold values from -6 to 6
- cotangent: bfloat16 [128, 196, 768], P(('dp', 'expert')), may hold values from -6 to 6
- gains: float32 [2, 768], replicated, may hold values from 0.5 to 1.5
- qkv_weight: bfloat16 [768, 2304], replicated, may hold values from -0.21875 to 0.21875
- out_weight: bfloat16 [768, 768], replicated, may hold values from -0.875 to 0.875
- router_weight: bfloat16 [768, 4], replicated, may hold values from -0.4375 to 0.4375
- up_weight: bfloat16 [4, 768, 3072], P('expert'), may hold values from -0.21875 to 0.21875
- down_weight: bfloat16 [4, 3072, 768], P('expert'), may hold values from -0.875 to 0.875
- choices: int32 [128, 196, 2], P(('dp', 'expert')), may hold values from 0 to 3, as said below
- slots: int32 [128, 196, 2], P(('dp', 'expert')), may hold values from -1 to 411, as said below
- owner_shared: int32 [16], replicated, may hold values from 0 to 15, as said below
- owner_expert: int32 [4, 32], P('expert'), may hold values from 0 to 31, as said below
- shared_m: float32 [16, 384, 384], P('dp')
- shared_v: float32 [16, 384, 384], P('dp'), as said below
- shared_left: float32 [16, 384, 384], P('dp'), may hold values from -1 to 1, as said below
- shared_right: float32 [16, 384, 384], P('dp'), may hold values from -1 to 1, as said below
- expert_m: float32 [4, 32, 384, 384], P('expert', 'dp')
- expert_v: float32 [4, 32, 384, 384], P('expert', 'dp'), as said below
- expert_left: float32 [4, 32, 384, 384], P('expert', 'dp'), may hold values from -1 to 1, as said below
- expert_right: float32 [4, 32, 384, 384], P('expert', 'dp'), may hold values from -1 to 1, as said below
- router_m: float32 [768, 4], replicated
- router_v: float32 [768, 4], replicated, as said below
- gains_m: float32 [2, 768], replicated
- gains_v: float32 [2, 768], replicated, as said below
Outputs:
- out: bfloat16 [128, 196, 768], P(('dp', 'expert'))
- grad_input: float32 [128, 196, 768], P(('dp', 'expert'))
- shared_m_new: float32 [16, 384, 384], P('dp')
- shared_v_new: float32 [16, 384, 384], P('dp')
- shared_w_new: float32 [16, 384, 384], P('dp')
- expert_m_new: float32 [4, 32, 384, 384], P('expert', 'dp')
- expert_v_new: float32 [4, 32, 384, 384], P('expert', 'dp')
- expert_w_new: float32 [4, 32, 384, 384], P('expert', 'dp')
- router_m_new: float32 [768, 4], replicated
- router_v_new: float32 [768, 4], replicated
- router_w_new: float32 [768, 4], replicated
- gains_m_new: float32 [2, 768], replicated
- gains_v_new: float32 [2, 768], replicated
- gains_w_new: float32 [2, 768], replicated
- qkv_copy: bfloat16 [768, 2304], replicated
- out_copy: bfloat16 [768, 768], replicated
- up_copy: bfloat16 [4, 768, 3072], P('expert')
- down_copy: bfloat16 [4, 3072, 768], P('expert')
The draws below stay inside these ranges and needn't reach their ends.
Inputs may be any that keep to these rules, and one draw needn't show every extreme that they name: `choices`: the two experts of a patch differ. `slots`: -1 marks a dropped pair. Within the pairs of one device's patches (aligned blocks of 784 patches) the places of one expert are 0, 1, 2, ... without gaps or repeats, given first to all first choices, then to second choices; a pair is dropped only when 412 places of its expert are taken. `owner_shared`: A permutation of the tiles. `owner_expert`: each row is a permutation of the tiles. `shared_left`: orthogonal matrices. `shared_right`: orthogonal matrices. `expert_left`: orthogonal matrices. `expert_right`: orthogonal matrices. `shared_v`: Positive. `expert_v`: Positive. `router_v`: Positive. `gains_v`: Positive.
All inputs are finite; a program needn't handle non-finite values.
Results may differ from the reference program's by a relative error of at most 0.023.
Values may be sent and summed in bfloat16 or wider, within the bound.
No kernel may reach another device: no remote copies, remote signals or barrier semaphores. Data moves between devices by JAX's collectives and lax.ppermute only.
A program may use at most 256 MiB of HBM per device.

```python
import math
from functools import partial
import jax
import jax.numpy as jnp
import numpy as np
from jax import lax

D = 768
HEADS = 12
HEAD_DIM = 64
FF = 3072
PATCHES = 196
IMG_DEV = 4
TILE = 384
SPECIALIST_COUNT = 4
IMAGES = 128
TOK_DEV = 784
TOKENS = 25088
SPECIALIST_SEATS = 412
NT_S = 16
NT_E = 32


def route_plan(key):
    base_key = jax.random.fold_in(key, 301)
    bias_key, noise_key, order_key = jax.random.split(base_key, 3)
    block_count = TOKENS // TOK_DEV
    dispatch_offset = jax.random.randint(bias_key, (SPECIALIST_COUNT,), 0, 4000)
    stochastic_perturbation = jax.random.randint(noise_key, (TOKENS, SPECIALIST_COUNT), 0, 8192)
    token_ids = jnp.arange(TOKENS, dtype=jnp.int32)
    resident_indices = token_ids % TOK_DEV
    imposed_selection = token_ids // TOK_DEV % SPECIALIST_COUNT
    specialist_indices = jnp.arange(SPECIALIST_COUNT, dtype=jnp.int32)
    preference_increment = jnp.where((resident_indices[:, None] < SPECIALIST_SEATS) & (specialist_indices[None, :] == imposed_selection[:, None]), 40000, 0)
    gating_logit_matrix = (stochastic_perturbation + dispatch_offset[None, :] + preference_increment) * SPECIALIST_COUNT + specialist_indices[None, :]
    ignored, picked = lax.top_k(gating_logit_matrix, 2)
    picked = picked.astype(jnp.int32)
    block_keys = jax.random.split(order_key, block_count)
    priority = jax.vmap(partial(permute_one, count=TOK_DEV))(block_keys).reshape(TOKENS)
    block_of = token_ids // TOK_DEV
    order_pos = jnp.stack([priority, priority + TOK_DEV], axis=1)
    flat_order = block_of[:, None] * (2 * TOK_DEV) + order_pos
    by_order = jnp.zeros((block_count * 2 * TOK_DEV,), jnp.int32).at[flat_order.reshape(-1)].set(picked.reshape(-1))
    by_order = by_order.reshape(block_count, 2 * TOK_DEV)
    onehot = (by_order[:, :, None] == specialist_indices[None, None, :]).astype(jnp.int32)
    running = jnp.cumsum(onehot, axis=1) - 1
    place_by_order = jnp.sum(running * onehot, axis=2).reshape(-1)
    places = place_by_order[flat_order]
    slot_values = jnp.where(places < SPECIALIST_SEATS, places, -1).astype(jnp.int32)
    return (picked, slot_values)


def permute_one(one_key, count):
    return jax.random.permutation(one_key, count).astype(jnp.int32)


def owner_lists(key, row_count, count, salt):
    key_list = jax.random.split(jax.random.fold_in(key, salt), row_count)
    return jax.vmap(partial(permute_one, count=count))(key_list)


def draw_choices(key, part):
    return route_plan(key)[0].reshape(IMAGES, PATCHES, 2)


def draw_slots(key, part):
    return route_plan(key)[1].reshape(IMAGES, PATCHES, 2)


def draw_owner_shared(key, part):
    return owner_lists(key, 1, NT_S, 401)[0]


def draw_owner_expert(key, part):
    return owner_lists(key, SPECIALIST_COUNT, NT_E, 402)


def first_draw(key, salt, shape, scales):
    normals = jax.random.truncated_normal(jax.random.fold_in(key, salt), -3.0, 3.0, shape, jnp.float32)
    return scales * normals


def second_draw(key, salt, shape, scales):
    spread = jax.random.uniform(jax.random.fold_in(key, salt), shape, jnp.float32, math.log(0.5), math.log(8.0))
    return scales * scales * jnp.exp(spread)


def expert_scales(key):
    kinds = owner_lists(key, SPECIALIST_COUNT, NT_E, 402) < NT_E // 2
    base_scale = math.sqrt(2.0 * TOKENS / SPECIALIST_COUNT)
    return jnp.where(kinds, 0.7 * base_scale, 0.2 * base_scale).astype(jnp.float32)[:, :, None, None]


def draw_shared_m(key, part):
    return first_draw(key, 501, (NT_S, TILE, TILE), 3.0 * math.sqrt(TOKENS))


def draw_shared_v(key, part):
    return second_draw(key, 502, (NT_S, TILE, TILE), 3.0 * math.sqrt(TOKENS))


def draw_expert_m(key, part):
    return first_draw(key, 503, (SPECIALIST_COUNT, NT_E, TILE, TILE), expert_scales(key))


def draw_expert_v(key, part):
    return second_draw(key, 504, (SPECIALIST_COUNT, NT_E, TILE, TILE), expert_scales(key))


def draw_router_m(key, part):
    return first_draw(key, 505, (D, SPECIALIST_COUNT), 20.0 * math.sqrt(TOKENS))


def draw_router_v(key, part):
    return second_draw(key, 506, (D, SPECIALIST_COUNT), 20.0 * math.sqrt(TOKENS))


def draw_gains_m(key, part):
    return first_draw(key, 507, (2, D), 6.0 * math.sqrt(TOKENS))


def draw_gains_v(key, part):
    return second_draw(key, 508, (2, D), 6.0 * math.sqrt(TOKENS))


def rotation_tables():
    segment = TILE // 3
    levels = segment.bit_length() - 1
    row_ids = np.arange(TILE)
    tables = []
    for level in range(levels):
        tables.append(row_ids ^ 1 << level)
    tables.append(np.where(row_ids < segment, row_ids + segment, np.where(row_ids < 2 * segment, row_ids - segment, row_ids)))
    tables.append(np.where(row_ids < segment, row_ids, np.where(row_ids < 2 * segment, row_ids + segment, row_ids - segment)))
    return (row_ids, tables)


def orthogonal(key, count):
    row_ids, tables = rotation_tables()
    angles = jax.random.uniform(key, (count, len(tables), TILE), jnp.float32, -math.pi, math.pi)
    result = jnp.broadcast_to(jnp.eye(TILE, dtype=jnp.float32), (count, TILE, TILE))
    for index, partner in enumerate(tables):
        lower = np.minimum(row_ids, partner)
        theta = angles[:, index, :][:, lower]
        sign_row = np.where(partner > row_ids, -1.0, np.where(partner < row_ids, 1.0, 0.0)).astype(np.float32)
        fixed_row = partner == row_ids
        cosine = jnp.where(fixed_row[None, :], 1.0, jnp.cos(theta))
        sine = jnp.sin(theta) * sign_row[None, :]
        result = cosine[:, :, None] * result + sine[:, :, None] * result[:, partner, :]
    return result


def draw_shared_left(key, part):
    return orthogonal(jax.random.fold_in(key, 601), NT_S)


def draw_shared_right(key, part):
    return orthogonal(jax.random.fold_in(key, 602), NT_S)


def draw_expert_left(key, part):
    return orthogonal(jax.random.fold_in(key, 603), SPECIALIST_COUNT * NT_E).reshape(SPECIALIST_COUNT, NT_E, TILE, TILE)


def draw_expert_right(key, part):
    return orthogonal(jax.random.fold_in(key, 604), SPECIALIST_COUNT * NT_E).reshape(SPECIALIST_COUNT, NT_E, TILE, TILE)


def block_scale(stream_key, shape, cuts, smallest, largest):
    def one(axis_at, shards_of):
        steps = jax.random.uniform(jax.random.fold_in(jax.random.fold_in(stream_key, 6), axis_at), (shards_of,), jnp.float32, smallest / len(cuts), largest / len(cuts))
        return jnp.repeat(jnp.exp(steps), shape[axis_at] // shards_of).reshape((-1,) + (1,) * (len(shape) - axis_at - 1))

    loudness = one(*cuts[0])
    for cut in cuts[1:]:
        loudness = loudness * one(*cut)
    return loudness


def scatter_about(key, extent, width, limit, shards=(), held_as=jnp.bfloat16):
    drawn = width * jax.random.normal(key, extent, jnp.float32)
    if shards:
        drawn = drawn * block_scale(key, extent, shards, -0.22, 0.18)
    return jnp.clip(drawn, -limit, limit).astype(held_as)


def setup_inputs(seed: int = 0) -> dict:
    seeds = jax.random.split(jax.random.key(seed), 25)
    return {
        "images": scatter_about(seeds[0], (IMAGES, PATCHES, D), 1.0, 6.0, ((0, 32),)),
        "cotangent": scatter_about(seeds[1], (IMAGES, PATCHES, D), 1.0, 6.0, ((0, 32),)),
        "gains": jnp.clip(1.0 + 0.1 * jax.random.normal(seeds[2], (2, D), jnp.float32), 0.5, 1.5),
        "qkv_weight": scatter_about(seeds[3], (D, 3 * D), D ** -0.5, 0.21875),
        "out_weight": scatter_about(seeds[4], (D, D), (D // 16) ** -0.5, 0.875),
        "router_weight": scatter_about(seeds[5], (D, SPECIALIST_COUNT), (D // 4) ** -0.5, 0.4375),
        "up_weight": scatter_about(seeds[6], (SPECIALIST_COUNT, D, FF), D ** -0.5, 0.21875, ((0, 4),)),
        "down_weight": scatter_about(seeds[7], (SPECIALIST_COUNT, FF, D), (FF // 64) ** -0.5, 0.875, ((0, 4),)),
        "choices": draw_choices(jax.random.fold_in(seeds[24], 71), 0),
        "slots": draw_slots(jax.random.fold_in(seeds[24], 71), 0),
        "owner_shared": draw_owner_shared(jax.random.fold_in(seeds[24], 71), 0),
        "owner_expert": draw_owner_expert(jax.random.fold_in(seeds[24], 71), 0),
        "shared_m": draw_shared_m(jax.random.fold_in(seeds[24], 71), 0),
        "shared_v": draw_shared_v(jax.random.fold_in(seeds[24], 71), 0),
        "shared_left": draw_shared_left(jax.random.fold_in(seeds[24], 71), 0),
        "shared_right": draw_shared_right(jax.random.fold_in(seeds[24], 71), 0),
        "expert_m": draw_expert_m(jax.random.fold_in(seeds[24], 71), 0),
        "expert_v": draw_expert_v(jax.random.fold_in(seeds[24], 71), 0),
        "expert_left": draw_expert_left(jax.random.fold_in(seeds[24], 71), 0),
        "expert_right": draw_expert_right(jax.random.fold_in(seeds[24], 71), 0),
        "router_m": draw_router_m(jax.random.fold_in(seeds[24], 71), 0),
        "router_v": draw_router_v(jax.random.fold_in(seeds[24], 71), 0),
        "gains_m": draw_gains_m(jax.random.fold_in(seeds[24], 71), 0),
        "gains_v": draw_gains_v(jax.random.fold_in(seeds[24], 71), 0),
    }


precise = lax.Precision.HIGHEST
norm_eps = 1e-06
adam_beta = 0.5
adam_eps = 1e-08
adam_step = 5
rate_scale = 0.3

@jax.custom_vjp
def low(v):
    return lax.optimization_barrier(v.astype(jnp.bfloat16)).astype(jnp.float32)

@jax.custom_vjp
def low_back(v):
    return v

def low_keep(v):
    return (low(v), None)

def low_pass(kept, grad):
    return (grad,)

def back_keep(v):
    return (v, None)

def back_low(kept, grad):
    return (low(grad),)
low.defvjp(low_keep, low_pass)
low_back.defvjp(back_keep, back_low)

def matmul(left_rows, right_rows):
    return jnp.dot(left_rows, right_rows, precision=precise, preferred_element_type=jnp.float32)

def layer_norm(values, gain_row):
    center = values - lax.optimization_barrier(jnp.mean(values, axis=-1, keepdims=True))
    variance = lax.optimization_barrier(jnp.mean(center * center, axis=-1, keepdims=True))
    return center * lax.rsqrt(variance + norm_eps) * gain_row

def attend_group(qkv_group):
    group_count = qkv_group.shape[0]
    split_heads = qkv_group.reshape(group_count, PATCHES, 3, HEADS, HEAD_DIM)
    queries = split_heads[:, :, 0]
    key_rows = split_heads[:, :, 1]
    value_rows = split_heads[:, :, 2]
    gating_logit_matrix = jnp.einsum('iqhd,ikhd->ihqk', queries, key_rows, precision=precise) * HEAD_DIM ** (-0.5)
    gating_logit_matrix = low_back(gating_logit_matrix)
    weights = jax.nn.softmax(gating_logit_matrix, axis=-1)
    mixed_rows = jnp.einsum('ihqk,ikhd->iqhd', low(weights), value_rows, precision=precise)
    return low(low_back(mixed_rows)).reshape(group_count, PATCHES, D)

def to_tiles(matrix):
    row_count = matrix.shape[-2]
    col_count = matrix.shape[-1]
    leading = matrix.shape[:-2]
    blocked = matrix.reshape(leading + (row_count // TILE, TILE, col_count // TILE, TILE))
    return jnp.swapaxes(blocked, -3, -2).reshape(leading + (-1, TILE, TILE))

def from_tiles(tiles, row_count, col_count):
    leading = tiles.shape[:-3]
    blocked = tiles.reshape(leading + (row_count // TILE, col_count // TILE, TILE, TILE))
    return jnp.swapaxes(blocked, -3, -2).reshape(leading + (row_count, col_count))

def rotated_adam(grad_tiles, weight_tiles, first_moment, second_moment, left_basis, right_basis):
    turned = jnp.einsum('...ji,...jk->...ik', left_basis, grad_tiles, precision=precise)
    turned = jnp.einsum('...ik,...kl->...il', turned, right_basis, precision=precise)
    first_new = adam_beta * first_moment + (1.0 - adam_beta) * turned
    second_new = adam_beta * second_moment + (1.0 - adam_beta) * turned * turned
    correction = 1.0 - adam_beta ** adam_step
    direction = first_new / correction / (jnp.sqrt(second_new / correction) + adam_eps)
    back_turn = jnp.einsum('...ij,...jk->...ik', left_basis, direction, precision=precise)
    back_turn = jnp.einsum('...ik,...lk->...il', back_turn, right_basis, precision=precise)
    step_rate = rate_scale * jnp.sqrt(lax.optimization_barrier(jnp.mean(weight_tiles * weight_tiles, axis=(-2, -1), keepdims=True)))
    return (first_new, second_new, weight_tiles - step_rate * back_turn)

def plain_adam(grad_values, weight_values, first_moment, second_moment, axes):
    first_new = adam_beta * first_moment + (1.0 - adam_beta) * grad_values
    second_new = adam_beta * second_moment + (1.0 - adam_beta) * grad_values * grad_values
    correction = 1.0 - adam_beta ** adam_step
    direction = first_new / correction / (jnp.sqrt(second_new / correction) + adam_eps)
    step_rate = rate_scale * jnp.sqrt(lax.optimization_barrier(jnp.mean(weight_values * weight_values, axis=axes, keepdims=True)))
    return (first_new, second_new, weight_values - step_rate * direction)

def reference(images, cotangent, gains, qkv_weight, out_weight, router_weight, up_weight, down_weight, choices, slots, owner_shared, owner_expert, shared_m, shared_v, shared_left, shared_right, expert_m, expert_v, expert_left, expert_right, router_m, router_v, gains_m, gains_v):
    block_count = TOKENS // TOK_DEV
    place_count = SPECIALIST_COUNT * block_count * SPECIALIST_SEATS
    choice_rows = choices.reshape(TOKENS, 2).astype(jnp.int32)
    slot_rows = slots.reshape(TOKENS, 2).astype(jnp.int32)
    kept_pairs = slot_rows >= 0
    block_index = (jnp.arange(TOKENS, dtype=jnp.int32) // TOK_DEV)[:, None]
    flat_place = jnp.where(kept_pairs, choice_rows * (block_count * SPECIALIST_SEATS) + block_index * SPECIALIST_SEATS + slot_rows, place_count).astype(jnp.int32)
    pair_ids = jnp.arange(2 * TOKENS, dtype=jnp.int32)
    pair_table = jnp.full((place_count + 1,), 2 * TOKENS, jnp.int32).at[flat_place.reshape(-1)].set(pair_ids)[:place_count]
    token_table = (pair_table // 2).astype(jnp.int32).reshape(SPECIALIST_COUNT, block_count * SPECIALIST_SEATS)

    def forward(image_rows, gain_rows, qkv_full, out_full, router_full, up_full, down_full):
        tokens = image_rows.reshape(TOKENS, D)
        normed = low(layer_norm(tokens, gain_rows[0]))
        qkv_all = low(low_back(matmul(normed, qkv_full)))
        grouped = qkv_all.reshape(IMAGES // IMG_DEV, IMG_DEV, PATCHES, 3 * D)
        attended = lax.map(jax.checkpoint(attend_group), grouped).reshape(TOKENS, D)
        hidden = tokens + low_back(matmul(attended, out_full))
        routed = low(layer_norm(hidden, gain_rows[1]))
        logits = low_back(matmul(routed, router_full))
        router_probs = jax.nn.softmax(logits, axis=-1)
        gate_values = jnp.where(kept_pairs, jnp.take_along_axis(router_probs, choice_rows, axis=1), 0.0)
        padded = jnp.concatenate([routed, jnp.zeros((1, D), jnp.float32)], axis=0)

        def expert_pass(operands):
            rows_index, up_one, down_one = operands
            expert_in = low_back(padded[rows_index])
            pre_act = low_back(matmul(expert_in, up_one))
            activated = low(jax.nn.gelu(pre_act, approximate=False))
            return low(low_back(matmul(activated, down_one)))
        expert_out = lax.map(jax.checkpoint(expert_pass), (token_table, up_full, down_full))
        flat_out = jnp.concatenate([expert_out.reshape(place_count, D), jnp.zeros((1, D), jnp.float32)], axis=0)
        pair_out = flat_out[flat_place]
        mixture = lax.optimization_barrier(jnp.sum(gate_values[:, :, None] * pair_out, axis=1))
        return (hidden + mixture).reshape(IMAGES, PATCHES, D)
    qkv_float = qkv_weight.astype(jnp.float32)
    out_float = out_weight.astype(jnp.float32)
    router_float = router_weight.astype(jnp.float32)
    up_float = up_weight.astype(jnp.float32)
    down_float = down_weight.astype(jnp.float32)
    result, pullback = jax.vjp(forward, images.astype(jnp.float32), gains, qkv_float, out_float, router_float, up_float, down_float)
    grad_images, grad_gains, grad_qkv, grad_out, grad_router, grad_up, grad_down = pullback(cotangent.astype(jnp.float32))
    out = result.astype(jnp.bfloat16)
    shared_grad = jnp.concatenate([to_tiles(grad_qkv), to_tiles(grad_out)], axis=0)[owner_shared]
    shared_old = jnp.concatenate([to_tiles(qkv_float), to_tiles(out_float)], axis=0)[owner_shared]
    shared_m_new, shared_v_new, shared_w_new = rotated_adam(shared_grad, shared_old, shared_m, shared_v, shared_left, shared_right)
    owner_index = owner_expert[:, :, None, None]
    expert_grad = jnp.take_along_axis(jnp.concatenate([to_tiles(grad_up), to_tiles(grad_down)], axis=1), owner_index, axis=1)
    expert_old = jnp.take_along_axis(jnp.concatenate([to_tiles(up_float), to_tiles(down_float)], axis=1), owner_index, axis=1)
    expert_m_new, expert_v_new, expert_w_new = rotated_adam(expert_grad, expert_old, expert_m, expert_v, expert_left, expert_right)
    router_m_new, router_v_new, router_w_new = plain_adam(grad_router, router_float, router_m, router_v, (0, 1))
    gains_m_new, gains_v_new, gains_w_new = plain_adam(grad_gains, gains, gains_m, gains_v, (1,))
    qkv_count = D // TILE * (3 * D // TILE)
    up_count = D // TILE * (FF // TILE)
    shared_inverse = jnp.zeros((NT_S,), jnp.int32).at[owner_shared].set(jnp.arange(NT_S, dtype=jnp.int32))
    shared_ordered = shared_w_new.astype(jnp.bfloat16)[shared_inverse]
    qkv_copy = from_tiles(shared_ordered[:qkv_count], D, 3 * D)
    out_copy = from_tiles(shared_ordered[qkv_count:], D, D)
    expert_rows = jnp.arange(SPECIALIST_COUNT, dtype=jnp.int32)[:, None]
    expert_inverse = jnp.zeros((SPECIALIST_COUNT, NT_E), jnp.int32).at[expert_rows, owner_expert].set(jnp.broadcast_to(jnp.arange(NT_E, dtype=jnp.int32)[None, :], (SPECIALIST_COUNT, NT_E)))
    expert_ordered = jnp.take_along_axis(expert_w_new.astype(jnp.bfloat16), expert_inverse[:, :, None, None], axis=1)
    up_copy = from_tiles(expert_ordered[:, :up_count], D, FF)
    down_copy = from_tiles(expert_ordered[:, up_count:], FF, D)
    return (out, grad_images, shared_m_new, shared_v_new, shared_w_new, expert_m_new, expert_v_new, expert_w_new, router_m_new, router_v_new, router_w_new, gains_m_new, gains_v_new, gains_w_new, qkv_copy, out_copy, up_copy, down_copy)
```

```python
import functools

import jax
import jax.numpy as jnp
from jax import lax
from jax.experimental import pallas as pl
from jax.experimental.pallas import tpu as pltpu
from jax.sharding import PartitionSpec as P

HEADS = 12
HEAD_DIM = 64
TILE = 384
LANES = 128
PAIRS = HEADS * HEAD_DIM // LANES

norm_eps = 1e-06
adam_beta = 0.5
adam_eps = 1e-08
adam_step = 5
rate_scale = 0.3
correction = 1.0 - adam_beta**adam_step
score_scale = HEAD_DIM ** (-0.5)

f32 = jnp.float32
bf16 = jnp.bfloat16
VMEM_LIMIT = 60 * 1024 * 1024


def round_up(value, step):
    return (value + step - 1) // step * step


def dot_nn(left, right):
    return lax.dot_general(left, right, (((1,), (0,)), ((), ())), preferred_element_type=f32)


def dot_nt(left, right):
    return lax.dot_general(left, right, (((1,), (1,)), ((), ())), preferred_element_type=f32)


def dot_tn(left, right):
    return lax.dot_general(left, right, (((0,), (0,)), ((), ())), preferred_element_type=f32)


def params(limit=VMEM_LIMIT):
    return pltpu.CompilerParams(vmem_limit_bytes=limit, dimension_semantics=("arbitrary",))


def norm_stats(values):
    center = values - jnp.mean(values, axis=-1, keepdims=True)
    inv_std = lax.rsqrt(jnp.mean(center * center, axis=-1, keepdims=True) + norm_eps)
    return center * inv_std, inv_std


def norm_back(grad_normed, unit_rows, inv_std, gain_row):
    grad_hat = grad_normed * gain_row
    gain_grad = jnp.sum(grad_normed * unit_rows, axis=0, keepdims=True)
    mean_one = jnp.mean(grad_hat, axis=-1, keepdims=True)
    mean_two = jnp.mean(grad_hat * unit_rows, axis=-1, keepdims=True)
    return inv_std * (grad_hat - mean_one - unit_rows * mean_two), gain_grad


def gelu_pair(x):
    t = 1.0 / (1.0 + 0.23164188 * jnp.abs(x))
    bell = jnp.exp(-0.5 * (x * x))
    poly = t * (
        0.127414796 + t * (-0.142248368 + t * (0.7107068705 + t * (-0.7265760135 + t * 0.5307027145)))
    )
    tail = poly * bell
    phi = jnp.where(x >= 0.0, 1.0 - tail, tail)
    return x * phi, phi + x * (bell * 0.3989422804014327)


def one_hot(columns, width):
    return jnp.where(
        columns == lax.broadcasted_iota(jnp.int32, (columns.shape[0], width), 1), 1.0, 0.0
    ).astype(bf16)


def full(shape):
    return pl.BlockSpec(shape, lambda i, *_: (0,) * len(shape))


def per(shape):
    return pl.BlockSpec((1,) + shape, lambda i, *_: (i,) + (0,) * len(shape))


def front_body(
    img, cot, gains, qkv_w, out_w, router_w, qkv_o, attn_o, mixed_o, hid_o, routed_o, probs_o, up_o, rows,
    *, patches, experts
):
    padded = rows.shape[0]
    rows[...] = jnp.zeros(rows.shape, f32)
    rows[0:patches, :] = cot[0].astype(f32)
    up_o[0] = rows[...].astype(bf16)
    rows[0:patches, :] = img[0].astype(f32)
    tokens = rows[...]
    unit, _ = norm_stats(tokens)
    normed = (unit * gains[0:1, :]).astype(bf16)
    qkv_o[0] = dot_nn(normed, qkv_w[...]).astype(bf16)
    width = PAIRS * LANES
    low_half = lax.broadcasted_iota(jnp.int32, (1, LANES), 1) < HEAD_DIM
    halves = (low_half.astype(f32).astype(bf16), (1.0 - low_half.astype(f32)).astype(bf16))
    key_bias = jnp.where(lax.broadcasted_iota(jnp.int32, (1, padded), 1) < patches, 0.0, -1e30)
    for pair in range(PAIRS):
        q = qkv_o[0, :, pair * LANES : (pair + 1) * LANES]
        k = qkv_o[0, :, width + pair * LANES : width + (pair + 1) * LANES]
        v = qkv_o[0, :, 2 * width + pair * LANES : 2 * width + (pair + 1) * LANES]
        outs = []
        for half in range(2):
            scores = dot_nt(q * halves[half], k) * score_scale + key_bias
            expo = jnp.exp(scores - jnp.max(scores, axis=-1, keepdims=True))
            low = (expo * (1.0 / jnp.sum(expo, axis=-1, keepdims=True))).astype(bf16)
            attn_o[0, 2 * pair + half] = low
            outs.append(dot_nn(low, v))
        mixed_o[0, :, pair * LANES : (pair + 1) * LANES] = jnp.where(low_half, outs[0], outs[1]).astype(bf16)
    hidden = rows[...] + dot_nn(mixed_o[0], out_w[...])
    hid_o[0] = hidden
    unit_two, _ = norm_stats(hidden)
    routed = (unit_two * gains[1:2, :]).astype(bf16)
    routed_o[0] = routed
    logits = dot_nn(routed, router_w[...])
    logits = jnp.where(lax.broadcasted_iota(jnp.int32, logits.shape, 1) < experts, logits, -1e30)
    expo = jnp.exp(logits - jnp.max(logits, axis=-1, keepdims=True))
    probs_o[0] = expo / jnp.sum(expo, axis=-1, keepdims=True)


def front(images, cotangent, gains, qkv_w, out_w, router_pad, experts, padded):
    count, patches, width = images.shape
    return pl.pallas_call(
        functools.partial(front_body, patches=patches, experts=experts),
        grid=(count,),
        in_specs=[
            per((patches, width)),
            per((patches, width)),
            full(gains.shape),
            full(qkv_w.shape),
            full(out_w.shape),
            full(router_pad.shape),
        ],
        out_specs=[
            per((padded, 3 * width)),
            per((HEADS, padded, padded)),
            per((padded, width)),
            per((padded, width)),
            per((padded, width)),
            per((padded, LANES)),
            per((padded, width)),
        ],
        out_shape=[
            jax.ShapeDtypeStruct((count, padded, 3 * width), bf16),
            jax.ShapeDtypeStruct((count, HEADS, padded, padded), bf16),
            jax.ShapeDtypeStruct((count, padded, width), bf16),
            jax.ShapeDtypeStruct((count, padded, width), f32),
            jax.ShapeDtypeStruct((count, padded, width), bf16),
            jax.ShapeDtypeStruct((count, padded, LANES), f32),
            jax.ShapeDtypeStruct((count, padded, width), bf16),
        ],
        scratch_shapes=[pltpu.VMEM((padded, width), f32)],
        compiler_params=params(),
        name="front",
    )(images, cotangent, gains, qkv_w, out_w, router_pad)


def dispatch_body(choice_rows, slot_rows, routed, probs, upstream, x_o, g_o):
    expert = pl.program_id(0)
    places = x_o.shape[1]
    tokens = routed.shape[0]
    slot = jnp.where(
        choice_rows[0:1, :] == expert,
        slot_rows[0:1, :],
        jnp.where(choice_rows[1:2, :] == expert, slot_rows[1:2, :], -1),
    )
    table = jnp.where(
        slot == lax.broadcasted_iota(jnp.int32, (places, tokens), 0), 1.0, 0.0
    ).astype(bf16)
    x_o[0] = dot_nn(table, routed[...]).astype(bf16)
    lane = lax.broadcasted_iota(jnp.int32, (1, LANES), 1)
    gate = jnp.sum(jnp.where(lane == expert, probs[...], 0.0), axis=-1, keepdims=True)
    gated = (gate * upstream[...].astype(f32)).astype(bf16)
    g_o[0] = dot_nn(table, gated).astype(bf16)


def dispatch(choice_rows, slot_rows, routed, probs, upstream, experts, places):
    width = routed.shape[1]
    shape = jax.ShapeDtypeStruct((experts, places, width), bf16)
    return pl.pallas_call(
        dispatch_body,
        grid=(experts,),
        in_specs=[full(a.shape) for a in (choice_rows, slot_rows, routed, probs, upstream)],
        out_specs=[per((places, width)), per((places, width))],
        out_shape=[shape, shape],
        compiler_params=params(),
        name="dispatch",
    )(choice_rows, slot_rows, routed, probs, upstream)


FF_CHUNK = 512


def ffn_fwd_body(x, up_w, down_w, act_o, slope_o, y_o):
    hidden = up_w.shape[2]
    total = None
    for start in range(0, hidden, FF_CHUNK):
        part = slice(start, start + FF_CHUNK)
        act, slope = gelu_pair(dot_nn(x[...], up_w[0, :, part]))
        act = act.astype(bf16)
        act_o[:, part] = act
        slope_o[:, part] = slope.astype(bf16)
        piece = dot_nn(act, down_w[0, part, :])
        total = piece if total is None else total + piece
    y_o[...] = total.astype(bf16)


def ffn_bwd_body(g, slope, up_w, down_w, pre_o, in_o):
    hidden = up_w.shape[2]
    total = None
    for start in range(0, hidden, FF_CHUNK):
        part = slice(start, start + FF_CHUNK)
        pre = (dot_nt(g[...], down_w[0, part, :]) * slope[:, part].astype(f32)).astype(bf16)
        pre_o[:, part] = pre
        piece = dot_nt(pre, up_w[0, :, part])
        total = piece if total is None else total + piece
    in_o[...] = total.astype(bf16)


def row_blocks(rows, width):
    return pl.BlockSpec((rows, width), lambda i: (i, 0))


def ffn_fwd(x, up_w, down_w):
    rows, width = x.shape
    hidden = up_w.shape[2]
    block = rows // 4
    return pl.pallas_call(
        ffn_fwd_body,
        grid=(4,),
        in_specs=[row_blocks(block, width), full(up_w.shape), full(down_w.shape)],
        out_specs=[row_blocks(block, hidden), row_blocks(block, hidden), row_blocks(block, width)],
        out_shape=[
            jax.ShapeDtypeStruct((rows, hidden), bf16),
            jax.ShapeDtypeStruct((rows, hidden), bf16),
            jax.ShapeDtypeStruct((rows, width), bf16),
        ],
        compiler_params=params(),
        name="ffn_fwd",
    )(x, up_w, down_w)


def ffn_bwd(g, slope, up_w, down_w):
    rows, width = g.shape
    hidden = up_w.shape[2]
    block = rows // 4
    return pl.pallas_call(
        ffn_bwd_body,
        grid=(4,),
        in_specs=[
            row_blocks(block, width),
            row_blocks(block, hidden),
            full(up_w.shape),
            full(down_w.shape),
        ],
        out_specs=[row_blocks(block, hidden), row_blocks(block, width)],
        out_shape=[
            jax.ShapeDtypeStruct((rows, hidden), bf16),
            jax.ShapeDtypeStruct((rows, width), bf16),
        ],
        compiler_params=params(),
        name="ffn_bwd",
    )(g, slope, up_w, down_w)


def expert_dw_body(owner, x, g, act, pre, tile_o, *, up_cols, down_cols, up_count):
    tile = owner[pl.program_id(0)]

    @pl.when(tile < up_count)
    def _():
        row = pl.multiple_of(tile // up_cols * TILE, TILE)
        tile_o[0] = dot_tn(x[:, pl.ds(row, TILE)], pre[...]).astype(bf16)

    @pl.when(tile >= up_count)
    def _():
        col = pl.multiple_of((tile - up_count) % down_cols * TILE, TILE)
        tile_o[0] = dot_tn(act[...], g[:, pl.ds(col, TILE)]).astype(bf16)


def expert_dw(owner, x, g, act, pre):
    rows, width = x.shape
    hidden = act.shape[1]
    up_cols = hidden // TILE
    down_cols = width // TILE
    up_count = up_cols * down_cols
    count = owner.shape[0]

    def pre_at(i, owner):
        tile = owner[i]
        return (0, jnp.where(tile < up_count, tile % up_cols, 0))

    def act_at(i, owner):
        tile = owner[i]
        return (0, jnp.where(tile >= up_count, (tile - up_count) // down_cols, 0))

    return pl.pallas_call(
        functools.partial(expert_dw_body, up_cols=up_cols, down_cols=down_cols, up_count=up_count),
        grid_spec=pltpu.PrefetchScalarGridSpec(
            num_scalar_prefetch=1,
            grid=(count,),
            in_specs=[
                full((rows, width)),
                full((rows, width)),
                pl.BlockSpec((rows, TILE), act_at),
                pl.BlockSpec((rows, TILE), pre_at),
            ],
            out_specs=per((TILE, TILE)),
        ),
        out_shape=jax.ShapeDtypeStruct((count, TILE, TILE), bf16),
        compiler_params=params(),
        name="expert_dw",
    )(owner, x, g, act, pre)


def combine_body(choice, slot, returned, hidden, upstream, probs, routed, out_o, logit_o, router_o, *, patches):
    experts, places = returned.shape[0], returned.shape[1]
    up = upstream[0].astype(f32)
    prob = probs[0]
    lane = lax.broadcasted_iota(jnp.int32, (1, LANES), 1)
    total = hidden[0]
    prob_grad = jnp.zeros(prob.shape, f32)
    for expert in range(experts):
        column = jnp.where(
            choice[0, :, 0:1] == expert,
            slot[0, :, 0:1],
            jnp.where(choice[0, :, 1:2] == expert, slot[0, :, 1:2], -1),
        )
        rows = dot_nn(one_hot(column, places), returned[expert])
        total = total + prob[:, expert : expert + 1] * rows
        prob_grad = prob_grad + jnp.where(
            lane == expert, jnp.sum(up * rows, axis=-1, keepdims=True), 0.0
        )
    out_o[0] = total[0:patches, :].astype(bf16)
    inner = jnp.sum(prob * prob_grad, axis=-1, keepdims=True)
    logit = (prob * (prob_grad - inner)).astype(bf16)
    logit_o[0] = logit

    @pl.when(pl.program_id(0) == 0)
    def _():
        router_o[...] = jnp.zeros(router_o.shape, f32)

    router_o[...] += dot_tn(logit, routed[0])


def combine(choice, slot, returned, hidden, upstream, probs, routed, patches):
    count, padded, width = hidden.shape
    return pl.pallas_call(
        functools.partial(combine_body, patches=patches),
        grid=(count,),
        in_specs=[
            per((padded, 2)),
            per((padded, 2)),
            full(returned.shape),
            per((padded, width)),
            per((padded, width)),
            per((padded, LANES)),
            per((padded, width)),
        ],
        out_specs=[per((patches, width)), per((padded, LANES)), full((LANES, width))],
        out_shape=[
            jax.ShapeDtypeStruct((count, patches, width), bf16),
            jax.ShapeDtypeStruct((count, padded, LANES), bf16),
            jax.ShapeDtypeStruct((LANES, width), f32),
        ],
        compiler_params=params(),
        name="combine",
    )(choice, slot, returned, hidden, upstream, probs, routed)


def back_body(
    owner, choice, slot, returned, logit, router_w, hidden, upstream, gains, out_w, mixed, qkv, attn, qkv_w, img,
    grad_o, tile_o, gain_o,
    rows, normed_all, qkv_grad_all, mixed_all, branch_all, mixed_grad_s, hidden_grad_s,
    *, patches, places
):
    image = pl.program_id(0)
    padded, width = rows.shape
    base = pl.multiple_of(image * padded, 16)
    here = pl.ds(base, padded)
    place = jnp.where(slot[0] >= 0, choice[0] * places + slot[0], -1)
    grid_places = lax.broadcasted_iota(jnp.int32, (padded, returned.shape[0]), 1)
    hits = (place[:, 0:1] == grid_places) | (place[:, 1:2] == grid_places)
    table = jnp.where(hits, 1.0, 0.0).astype(bf16)
    routed_grad = dot_nt(logit[0], router_w[...]) + dot_nn(table, returned[...])
    unit_two, inv_two = norm_stats(hidden[0])
    norm_grad, gain_two = norm_back(routed_grad, unit_two, inv_two, gains[1:2, :])
    hidden_grad = upstream[0].astype(f32) + norm_grad
    hidden_grad_s[...] = hidden_grad
    branch = hidden_grad.astype(bf16)
    branch_all[here, :] = branch
    mixed_all[here, :] = mixed[0]
    mixed_grad_s[...] = dot_nt(branch, out_w[...]).astype(bf16)
    low_half = lax.broadcasted_iota(jnp.int32, (1, LANES), 1) < HEAD_DIM
    halves = (low_half.astype(f32).astype(bf16), (1.0 - low_half.astype(f32)).astype(bf16))
    for pair in range(PAIRS):
        cols = slice(pair * LANES, (pair + 1) * LANES)
        q = qkv[0, :, pair * LANES : (pair + 1) * LANES]
        k = qkv[0, :, width + pair * LANES : width + (pair + 1) * LANES]
        v = qkv[0, :, 2 * width + pair * LANES : 2 * width + (pair + 1) * LANES]
        mg = mixed_grad_s[:, cols]
        q_grads, k_grads, v_grads = [], [], []
        for half in range(2):
            low = attn[0, 2 * pair + half]
            weights = low.astype(f32)
            weight_grad = dot_nt(mg * halves[half], v)
            product = weights * weight_grad
            inner = jnp.sum(product, axis=-1, keepdims=True)
            score = (product - weights * inner).astype(bf16)
            q_grads.append(dot_nn(score, k))
            k_grads.append(dot_tn(score, q))
            v_grads.append(dot_tn(low, mg))
        qkv_grad_all[here, pair * LANES : (pair + 1) * LANES] = (
            jnp.where(low_half, q_grads[0], q_grads[1]) * score_scale
        ).astype(bf16)
        qkv_grad_all[here, width + pair * LANES : width + (pair + 1) * LANES] = (
            jnp.where(low_half, k_grads[0], k_grads[1]) * score_scale
        ).astype(bf16)
        qkv_grad_all[here, 2 * width + pair * LANES : 2 * width + (pair + 1) * LANES] = jnp.where(
            low_half, v_grads[0], v_grads[1]
        ).astype(bf16)
    rows[...] = jnp.zeros(rows.shape, f32)
    rows[0:patches, :] = img[0].astype(f32)
    unit_one, inv_one = norm_stats(rows[...])
    normed_all[here, :] = (unit_one * gains[0:1, :]).astype(bf16)
    normed_grad = dot_nt(qkv_grad_all[here, :], qkv_w[...])
    norm_grad_one, gain_one = norm_back(normed_grad, unit_one, inv_one, gains[0:1, :])
    grad_o[0] = (hidden_grad_s[...] + norm_grad_one)[0:patches, :]

    @pl.when(image == 0)
    def _():
        gain_o[...] = jnp.zeros(gain_o.shape, f32)

    gain_o[0:1, :] += gain_one
    gain_o[1:2, :] += gain_two

    @pl.when(image == pl.num_programs(0) - 1)
    def _():
        row_tiles = width // TILE
        qkv_cols = 3 * row_tiles
        qkv_count = row_tiles * qkv_cols

        def one(s, carry):
            tile = owner[s]

            @pl.when(tile < qkv_count)
            def _():
                row = pl.multiple_of(tile // qkv_cols * TILE, TILE)
                col = pl.multiple_of(tile % qkv_cols * TILE, TILE)
                tile_o[s] = dot_tn(
                    normed_all[:, pl.ds(row, TILE)], qkv_grad_all[:, pl.ds(col, TILE)]
                ).astype(bf16)

            @pl.when(tile >= qkv_count)
            def _():
                rest = tile - qkv_count
                row = pl.multiple_of(rest // row_tiles * TILE, TILE)
                col = pl.multiple_of(rest % row_tiles * TILE, TILE)
                tile_o[s] = dot_tn(
                    mixed_all[:, pl.ds(row, TILE)], branch_all[:, pl.ds(col, TILE)]
                ).astype(bf16)

            return carry

        lax.fori_loop(0, tile_o.shape[0], one, 0)


def back(owner, choice, slot, returned, logit, router_pad, hidden, upstream, gains, out_w, mixed, qkv, attn, qkv_w,
         images, places):
    count, patches, width = images.shape
    padded = hidden.shape[1]
    tiles = owner.shape[0]
    return pl.pallas_call(
        functools.partial(back_body, patches=patches, places=places),
        grid_spec=pltpu.PrefetchScalarGridSpec(
            num_scalar_prefetch=1,
            grid=(count,),
            in_specs=[
                per((padded, 2)),
                per((padded, 2)),
                full(returned.shape),
                per((padded, LANES)),
                full(router_pad.shape),
                per((padded, width)),
                per((padded, width)),
                full(gains.shape),
                full(out_w.shape),
                per((padded, width)),
                per((padded, 3 * width)),
                per((HEADS, padded, padded)),
                full(qkv_w.shape),
                per((patches, width)),
            ],
            out_specs=[per((patches, width)), full((tiles, TILE, TILE)), full((8, width))],
            scratch_shapes=[
                pltpu.VMEM((padded, width), f32),
                pltpu.VMEM((count * padded, width), bf16),
                pltpu.VMEM((count * padded, 3 * width), bf16),
                pltpu.VMEM((count * padded, width), bf16),
                pltpu.VMEM((count * padded, width), bf16),
                pltpu.VMEM((padded, width), bf16),
                pltpu.VMEM((padded, width), f32),
            ],
        ),
        out_shape=[
            jax.ShapeDtypeStruct((count, patches, width), f32),
            jax.ShapeDtypeStruct((tiles, TILE, TILE), bf16),
            jax.ShapeDtypeStruct((8, width), f32),
        ],
        compiler_params=params(),
        name="back",
    )(owner, choice, slot, returned, logit, router_pad, hidden, upstream, gains, out_w, mixed, qkv, attn, qkv_w, images)


def adam_body(owner, grad, w_one, w_two, m, v, left, right, m_o, v_o, w_o, low_o, *, first_count):
    tile = owner[pl.program_id(0)]
    first = (tile < first_count).astype(f32)
    old = w_one[...].astype(f32) * first + w_two[...].astype(f32) * (1.0 - first)
    left_low = left[0].astype(bf16)
    right_low = right[0].astype(bf16)
    turned = dot_nn(dot_tn(left_low, grad[0].astype(bf16)).astype(bf16), right_low)
    m_new = adam_beta * m[0] + (1.0 - adam_beta) * turned
    v_new = adam_beta * v[0] + (1.0 - adam_beta) * turned * turned
    m_o[0] = m_new
    v_o[0] = v_new
    direction = m_new / correction / (jnp.sqrt(v_new / correction) + adam_eps)
    back_turn = dot_nt(dot_nn(left_low, direction.astype(bf16)).astype(bf16), right_low)
    rate = rate_scale * jnp.sqrt(jnp.mean(old * old))
    new = old - rate * back_turn
    w_o[0] = new
    low_o[0] = new.astype(bf16)


def rotated_adam(owner, grad, w_one, w_two, m, v, left, right):
    count = m.shape[0]
    one_cols = w_one.shape[1] // TILE
    two_cols = w_two.shape[1] // TILE
    first_count = w_one.shape[0] // TILE * one_cols

    def one_at(i, owner):
        tile = jnp.minimum(owner[i], first_count - 1)
        return (tile // one_cols, tile % one_cols)

    def two_at(i, owner):
        tile = jnp.maximum(owner[i] - first_count, 0)
        return (tile // two_cols, tile % two_cols)

    spec = per((TILE, TILE))
    shape = jax.ShapeDtypeStruct((count, TILE, TILE), f32)
    return pl.pallas_call(
        functools.partial(adam_body, first_count=first_count),
        grid_spec=pltpu.PrefetchScalarGridSpec(
            num_scalar_prefetch=1,
            grid=(count,),
            in_specs=[
                spec,
                pl.BlockSpec((TILE, TILE), one_at),
                pl.BlockSpec((TILE, TILE), two_at),
                spec,
                spec,
                spec,
                spec,
            ],
            out_specs=[spec, spec, spec, spec],
        ),
        out_shape=[shape, shape, shape, jax.ShapeDtypeStruct((count, TILE, TILE), bf16)],
        compiler_params=params(),
        name="adam",
    )(owner, grad, w_one, w_two, m, v, left, right)


def untile_body(slot_of, tile, out):
    out[...] = tile[0]


def untile(slot_of, tiles, row_count, col_count):
    cols = col_count // TILE
    count = slot_of.shape[0]
    return pl.pallas_call(
        untile_body,
        grid_spec=pltpu.PrefetchScalarGridSpec(
            num_scalar_prefetch=1,
            grid=(count,),
            in_specs=[pl.BlockSpec((1, TILE, TILE), lambda i, slot_of: (slot_of[i], 0, 0))],
            out_specs=pl.BlockSpec((TILE, TILE), lambda i, slot_of: (i // cols, i % cols)),
        ),
        out_shape=jax.ShapeDtypeStruct((row_count, col_count), bf16),
        compiler_params=params(),
        name="untile",
    )(slot_of, tiles)


def inverse(owner):
    ids = jnp.arange(owner.shape[0], dtype=jnp.int32)
    return jnp.sum(jnp.where(owner[None, :] == ids[:, None], ids[None, :], 0), axis=1)


def plain_adam(grad_values, weight_values, first_moment, second_moment, axes):
    first_new = adam_beta * first_moment + (1.0 - adam_beta) * grad_values
    second_new = adam_beta * second_moment + (1.0 - adam_beta) * grad_values * grad_values
    direction = first_new / correction / (jnp.sqrt(second_new / correction) + adam_eps)
    step_rate = rate_scale * jnp.sqrt(
        jnp.mean(weight_values * weight_values, axis=axes, keepdims=True)
    )
    return (first_new, second_new, weight_values - step_rate * direction)


def shards(
    images,
    cotangent,
    gains,
    qkv_weight,
    out_weight,
    router_weight,
    up_weight,
    down_weight,
    choices,
    slots,
    owner_shared,
    owner_expert,
    shared_m,
    shared_v,
    shared_left,
    shared_right,
    expert_m,
    expert_v,
    expert_left,
    expert_right,
    router_m,
    router_v,
    gains_m,
    gains_v,
):
    count, patches, width = images.shape
    hidden_width = up_weight.shape[2]
    experts = router_weight.shape[1]
    dp_size = lax.axis_size("dp")
    dp_index = lax.axis_index("dp")
    capacity = (42 * count * patches + 20 * experts - 1) // (20 * experts)
    places = round_up(capacity, 16)
    padded = round_up(patches, 16)
    tokens = count * padded
    router_pad = jnp.pad(router_weight, ((0, 0), (0, LANES - experts)))
    spare = ((0, 0), (0, padded - patches), (0, 0))
    choice = jnp.pad(choices, spare)
    slot = jnp.pad(slots, spare, constant_values=-1)
    choice_rows = choice.reshape(tokens, 2).T
    slot_rows = slot.reshape(tokens, 2).T

    qkv, attn, mixed, hidden, routed, probs, upstream = front(
        images, cotangent, gains, qkv_weight, out_weight, router_pad, experts, padded
    )
    outgoing, outgoing_grad = dispatch(
        choice_rows,
        slot_rows,
        routed.reshape(tokens, width),
        probs.reshape(tokens, LANES),
        upstream.reshape(tokens, width),
        experts,
        places,
    )

    def exchange(rows):
        return lax.all_to_all(rows, "expert", split_axis=0, concat_axis=0, tiled=True)

    total_places = experts * places
    arriving = exchange(outgoing).reshape(total_places, width)
    arriving_grad = exchange(outgoing_grad).reshape(total_places, width)
    act, slope, produced = ffn_fwd(arriving, up_weight, down_weight)
    returned = exchange(produced.reshape(experts, places, width))
    pre_grad, in_grad = ffn_bwd(arriving_grad, slope, up_weight, down_weight)
    returned_grad = exchange(in_grad.reshape(experts, places, width)).reshape(total_places, width)
    owner_row = owner_expert[0]
    expert_grads = expert_dw(owner_row, arriving, arriving_grad, act, pre_grad)
    expert_own = lax.psum_scatter(expert_grads, "dp", scatter_dimension=0, tiled=True)
    out, logit_low, router_grad = combine(
        choice, slot, returned, hidden, upstream, probs, routed, patches
    )
    grad_input, shared_grads, gain_grads = back(
        owner_shared, choice, slot, returned_grad, logit_low, router_pad, hidden, upstream, gains, out_weight,
        mixed, qkv, attn, qkv_weight, images, places,
    )
    shared_part = lax.psum_scatter(shared_grads, "dp", scatter_dimension=0, tiled=True)
    shared_own = lax.psum(shared_part, "expert")
    small = lax.psum(
        jnp.concatenate([router_grad[: round_up(experts, 8)], gain_grads], axis=0), ("dp", "expert")
    )
    router_total = small[:experts].T
    gains_total = small[round_up(experts, 8) : round_up(experts, 8) + 2]

    own_shared = owner_shared.shape[0] // dp_size
    own_expert = owner_row.shape[0] // dp_size
    my_shared = lax.dynamic_slice_in_dim(owner_shared, dp_index * own_shared, own_shared)
    my_expert = lax.dynamic_slice_in_dim(owner_row, dp_index * own_expert, own_expert)
    expert_m_new, expert_v_new, expert_w_new, expert_low = rotated_adam(
        my_expert, expert_own, up_weight[0], down_weight[0],
        expert_m[0], expert_v[0], expert_left[0], expert_right[0],
    )
    expert_all = lax.all_gather(expert_low, "dp", axis=0, tiled=True)
    shared_m_new, shared_v_new, shared_w_new, shared_low = rotated_adam(
        my_shared, shared_own, qkv_weight, out_weight, shared_m, shared_v, shared_left, shared_right
    )
    shared_all = lax.all_gather(shared_low, "dp", axis=0, tiled=True)
    router_m_new, router_v_new, router_w_new = plain_adam(
        router_total, router_weight.astype(f32), router_m, router_v, (0, 1)
    )
    gains_m_new, gains_v_new, gains_w_new = plain_adam(gains_total, gains, gains_m, gains_v, (1,))

    expert_slot = inverse(owner_row)
    shared_slot = inverse(owner_shared)
    up_count = (width // TILE) * (hidden_width // TILE)
    qkv_count = (width // TILE) * (3 * width // TILE)
    up_copy = untile(expert_slot[:up_count], expert_all, width, hidden_width)
    down_copy = untile(expert_slot[up_count:], expert_all, hidden_width, width)
    qkv_copy = untile(shared_slot[:qkv_count], shared_all, width, 3 * width)
    out_copy = untile(shared_slot[qkv_count:], shared_all, width, width)
    return (
        out,
        grad_input,
        shared_m_new,
        shared_v_new,
        shared_w_new,
        expert_m_new[None],
        expert_v_new[None],
        expert_w_new[None],
        router_m_new,
        router_v_new,
        router_w_new,
        gains_m_new,
        gains_v_new,
        gains_w_new,
        qkv_copy,
        out_copy,
        up_copy[None],
        down_copy[None],
    )


def solution(mesh):
    rows = P(("dp", "expert"), None, None)
    shared = P("dp", None, None)
    expert = P("expert", "dp", None, None)
    weight = P("expert", None, None)
    return jax.shard_map(
        shards,
        mesh=mesh,
        in_specs=(
            (rows, rows) + (P(),) * 4 + (weight, weight, rows, rows, P(), P("expert", None))
            + (shared,) * 4 + (expert,) * 4 + (P(),) * 4
        ),
        out_specs=(
            (rows, rows) + (shared,) * 3 + (expert,) * 3 + (P(),) * 8 + (weight, weight)
        ),
        check_vma=False,
    )
```

```python
import functools

import jax
import jax.numpy as jnp
from jax import lax
from jax.experimental import pallas as pl
from jax.experimental.pallas import tpu as pltpu
from jax.sharding import PartitionSpec as P


HEADS = 12
HEAD_DIM = 64
TILE = 384
LANES = 128
PAIRS = HEADS * HEAD_DIM // LANES

norm_eps = 1e-06
adam_beta = 0.5
adam_eps = 1e-08
adam_step = 5
rate_scale = 0.3
correction = 1.0 - adam_beta**adam_step
score_scale = HEAD_DIM ** (-0.5)

f32 = jnp.float32
bf16 = jnp.bfloat16
VMEM_LIMIT = 60 * 1024 * 1024


def round_up(value, step):
    return (value + step - 1) // step * step


def dot_nn(left, right):
    return lax.dot_general(left, right, (((1,), (0,)), ((), ())), preferred_element_type=f32)


def dot_nt(left, right):
    return lax.dot_general(left, right, (((1,), (1,)), ((), ())), preferred_element_type=f32)


def dot_tn(left, right):
    return lax.dot_general(left, right, (((0,), (0,)), ((), ())), preferred_element_type=f32)


def params(limit=VMEM_LIMIT):
    return pltpu.CompilerParams(vmem_limit_bytes=limit, dimension_semantics=("arbitrary",))


def norm_stats(values):
    center = values - jnp.mean(values, axis=-1, keepdims=True)
    inv_std = lax.rsqrt(jnp.mean(center * center, axis=-1, keepdims=True) + norm_eps)
    return center * inv_std, inv_std


def norm_back(grad_normed, unit_rows, inv_std, gain_row):
    grad_hat = grad_normed * gain_row
    gain_grad = jnp.sum(grad_normed * unit_rows, axis=0, keepdims=True)
    mean_one = jnp.mean(grad_hat, axis=-1, keepdims=True)
    mean_two = jnp.mean(grad_hat * unit_rows, axis=-1, keepdims=True)
    return inv_std * (grad_hat - mean_one - unit_rows * mean_two), gain_grad


def gelu_pair(x):
    t = 1.0 / (1.0 + 0.23164188 * jnp.abs(x))
    bell = jnp.exp(-0.5 * (x * x))
    poly = t * (
        0.127414796 + t * (-0.142248368 + t * (0.7107068705 + t * (-0.7265760135 + t * 0.5307027145)))
    )
    tail = poly * bell
    phi = jnp.where(x >= 0.0, 1.0 - tail, tail)
    return x * phi, phi + x * (bell * 0.3989422804014327)


def one_hot(columns, width):
    return jnp.where(
        columns == lax.broadcasted_iota(jnp.int32, (columns.shape[0], width), 1), 1.0, 0.0
    ).astype(bf16)


def full(shape):
    return pl.BlockSpec(shape, lambda i, *_: (0,) * len(shape))


def per(shape):
    return pl.BlockSpec((1,) + shape, lambda i, *_: (i,) + (0,) * len(shape))


def front_body(
    img, cot, gains, qkv_w, out_w, router_w, qkv_o, attn_o, mixed_o, hid_o, routed_o, probs_o, up_o, rows,
    *, patches, experts
):
    padded = rows.shape[0]
    rows[...] = jnp.zeros(rows.shape, f32)
    rows[0:patches, :] = cot[0].astype(f32)
    up_o[0] = rows[...].astype(bf16)
    rows[0:patches, :] = img[0].astype(f32)
    tokens = rows[...]
    unit, _ = norm_stats(tokens)
    normed = (unit * gains[0:1, :]).astype(bf16)
    qkv_o[0] = dot_nn(normed, qkv_w[...]).astype(bf16)
    width = PAIRS * LANES
    low_half = lax.broadcasted_iota(jnp.int32, (1, LANES), 1) < HEAD_DIM
    halves = (low_half.astype(f32).astype(bf16), (1.0 - low_half.astype(f32)).astype(bf16))
    key_bias = jnp.where(lax.broadcasted_iota(jnp.int32, (1, padded), 1) < patches, 0.0, -1e30)
    for pair in range(PAIRS):
        q = qkv_o[0, :, pair * LANES : (pair + 1) * LANES]
        k = qkv_o[0, :, width + pair * LANES : width + (pair + 1) * LANES]
        v = qkv_o[0, :, 2 * width + pair * LANES : 2 * width + (pair + 1) * LANES]
        outs = []
        for half in range(2):
            scores = dot_nt(q * halves[half], k) * score_scale + key_bias
            expo = jnp.exp(scores - jnp.max(scores, axis=-1, keepdims=True))
            low = (expo * (1.0 / jnp.sum(expo, axis=-1, keepdims=True))).astype(bf16)
            attn_o[0, 2 * pair + half] = low
            outs.append(dot_nn(low, v))
        mixed_o[0, :, pair * LANES : (pair + 1) * LANES] = jnp.where(low_half, outs[0], outs[1]).astype(bf16)
    hidden = rows[...] + dot_nn(mixed_o[0], out_w[...])
    hid_o[0] = hidden
    unit_two, _ = norm_stats(hidden)
    routed = (unit_two * gains[1:2, :]).astype(bf16)
    routed_o[0] = routed
    logits = dot_nn(routed, router_w[...])
    logits = jnp.where(lax.broadcasted_iota(jnp.int32, logits.shape, 1) < experts, logits, -1e30)
    expo = jnp.exp(logits - jnp.max(logits, axis=-1, keepdims=True))
    probs_o[0] = expo / jnp.sum(expo, axis=-1, keepdims=True)


def front(images, cotangent, gains, qkv_w, out_w, router_pad, experts, padded):
    count, patches, width = images.shape
    return pl.pallas_call(
        functools.partial(front_body, patches=patches, experts=experts),
        grid=(count,),
        in_specs=[
            per((patches, width)),
            per((patches, width)),
            full(gains.shape),
            full(qkv_w.shape),
            full(out_w.shape),
            full(router_pad.shape),
        ],
        out_specs=[
            per((padded, 3 * width)),
            per((HEADS, padded, padded)),
            per((padded, width)),
            per((padded, width)),
            per((padded, width)),
            per((padded, LANES)),
            per((padded, width)),
        ],
        out_shape=[
            jax.ShapeDtypeStruct((count, padded, 3 * width), bf16),
            jax.ShapeDtypeStruct((count, HEADS, padded, padded), bf16),
            jax.ShapeDtypeStruct((count, padded, width), bf16),
            jax.ShapeDtypeStruct((count, padded, width), f32),
            jax.ShapeDtypeStruct((count, padded, width), bf16),
            jax.ShapeDtypeStruct((count, padded, LANES), f32),
            jax.ShapeDtypeStruct((count, padded, width), bf16),
        ],
        scratch_shapes=[pltpu.VMEM((padded, width), f32)],
        compiler_params=params(),
        name="front",
    )(images, cotangent, gains, qkv_w, out_w, router_pad)


def dispatch_body(choice_rows, slot_rows, routed, probs, upstream, x_o, g_o):
    expert = pl.program_id(0)
    places = x_o.shape[1]
    tokens = routed.shape[0]
    slot = jnp.where(
        choice_rows[0:1, :] == expert,
        slot_rows[0:1, :],
        jnp.where(choice_rows[1:2, :] == expert, slot_rows[1:2, :], -1),
    )
    table = jnp.where(
        slot == lax.broadcasted_iota(jnp.int32, (places, tokens), 0), 1.0, 0.0
    ).astype(bf16)
    x_o[0] = dot_nn(table, routed[...]).astype(bf16)
    lane = lax.broadcasted_iota(jnp.int32, (1, LANES), 1)
    gate = jnp.sum(jnp.where(lane == expert, probs[...], 0.0), axis=-1, keepdims=True)
    gated = (gate * upstream[...].astype(f32)).astype(bf16)
    g_o[0] = dot_nn(table, gated).astype(bf16)


def dispatch(choice_rows, slot_rows, routed, probs, upstream, experts, places):
    width = routed.shape[1]
    shape = jax.ShapeDtypeStruct((experts, places, width), bf16)
    return pl.pallas_call(
        dispatch_body,
        grid=(experts,),
        in_specs=[full(a.shape) for a in (choice_rows, slot_rows, routed, probs, upstream)],
        out_specs=[per((places, width)), per((places, width))],
        out_shape=[shape, shape],
        compiler_params=params(),
        name="dispatch",
    )(choice_rows, slot_rows, routed, probs, upstream)


FF_CHUNK = 512


def ffn_fwd_body(x, up_w, down_w, act_o, slope_o, y_o):
    hidden = up_w.shape[2]
    total = None
    for start in range(0, hidden, FF_CHUNK):
        part = slice(start, start + FF_CHUNK)
        act, slope = gelu_pair(dot_nn(x[...], up_w[0, :, part]))
        act = act.astype(bf16)
        act_o[:, part] = act
        slope_o[:, part] = slope.astype(bf16)
        piece = dot_nn(act, down_w[0, part, :])
        total = piece if total is None else total + piece
    y_o[...] = total.astype(bf16)


def ffn_bwd_body(g, slope, up_w, down_w, pre_o, in_o):
    hidden = up_w.shape[2]
    total = None
    for start in range(0, hidden, FF_CHUNK):
        part = slice(start, start + FF_CHUNK)
        pre = (dot_nt(g[...], down_w[0, part, :]) * slope[:, part].astype(f32)).astype(bf16)
        pre_o[:, part] = pre
        piece = dot_nt(pre, up_w[0, :, part])
        total = piece if total is None else total + piece
    in_o[...] = total.astype(bf16)


def row_blocks(rows, width):
    return pl.BlockSpec((rows, width), lambda i: (i, 0))


def ffn_fwd(x, up_w, down_w):
    rows, width = x.shape
    hidden = up_w.shape[2]
    block = rows // 4
    return pl.pallas_call(
        ffn_fwd_body,
        grid=(4,),
        in_specs=[row_blocks(block, width), full(up_w.shape), full(down_w.shape)],
        out_specs=[row_blocks(block, hidden), row_blocks(block, hidden), row_blocks(block, width)],
        out_shape=[
            jax.ShapeDtypeStruct((rows, hidden), bf16),
            jax.ShapeDtypeStruct((rows, hidden), bf16),
            jax.ShapeDtypeStruct((rows, width), bf16),
        ],
        compiler_params=params(),
        name="ffn_fwd",
    )(x, up_w, down_w)


def ffn_bwd(g, slope, up_w, down_w):
    rows, width = g.shape
    hidden = up_w.shape[2]
    block = rows // 4
    return pl.pallas_call(
        ffn_bwd_body,
        grid=(4,),
        in_specs=[
            row_blocks(block, width),
            row_blocks(block, hidden),
            full(up_w.shape),
            full(down_w.shape),
        ],
        out_specs=[row_blocks(block, hidden), row_blocks(block, width)],
        out_shape=[
            jax.ShapeDtypeStruct((rows, hidden), bf16),
            jax.ShapeDtypeStruct((rows, width), bf16),
        ],
        compiler_params=params(),
        name="ffn_bwd",
    )(g, slope, up_w, down_w)


def turn(rows):
    width = rows.shape[1]
    same = lax.broadcasted_iota(jnp.int32, (width, width), 0) == lax.broadcasted_iota(
        jnp.int32, (width, width), 1
    )
    return dot_nt(jnp.where(same, 1.0, 0.0).astype(bf16), rows).astype(bf16)


DW_CHUNK = 2 * TILE


def expert_dw_body(slot_of, x, g, act, pre, after, tile_o, x_turned, g_turned, *, up_cols, down_cols):
    step = pl.program_id(0)

    @pl.when(step == 0)
    def _():
        x_turned[...] = turn(x[...])
        g_turned[...] = turn(g[...])

    up_count = up_cols * down_cols
    part = dot_nn(x_turned[...], pre[...]).astype(bf16)
    for row in range(down_cols):
        for col in range(2):
            slot = slot_of[row * up_cols + 2 * step + col]
            tile_o[slot] = part[row * TILE : (row + 1) * TILE, col * TILE : (col + 1) * TILE]
    part = dot_nn(g_turned[...], act[...]).astype(bf16)
    for row in range(2):
        for col in range(down_cols):
            slot = slot_of[up_count + (2 * step + row) * down_cols + col]
            tile_o[slot] = part[col * TILE : (col + 1) * TILE, row * TILE : (row + 1) * TILE].T


def expert_dw(slot_of, x, g, act, pre, after):
    rows, width = x.shape
    hidden = act.shape[1]
    count = slot_of.shape[0]
    columns = pl.BlockSpec((rows, DW_CHUNK), lambda i, slot_of: (0, i))
    return pl.pallas_call(
        functools.partial(expert_dw_body, up_cols=hidden // TILE, down_cols=width // TILE),
        grid_spec=pltpu.PrefetchScalarGridSpec(
            num_scalar_prefetch=1,
            grid=(hidden // DW_CHUNK,),
            in_specs=[
                full((rows, width)),
                full((rows, width)),
                columns,
                columns,
                pl.BlockSpec(memory_space=pl.ANY),
            ],
            out_specs=full((count, TILE, TILE)),
            scratch_shapes=[pltpu.VMEM((width, rows), bf16), pltpu.VMEM((width, rows), bf16)],
        ),
        out_shape=jax.ShapeDtypeStruct((count, TILE, TILE), bf16),
        compiler_params=params(),
        name="expert_dw",
    )(slot_of, x, g, act, pre, after)


def combine_body(choice, slot, returned, hidden, upstream, probs, routed, after, later, out_o, logit_o, router_o, *, patches):
    experts, places = returned.shape[0], returned.shape[1]
    up = upstream[0].astype(f32)
    prob = probs[0]
    lane = lax.broadcasted_iota(jnp.int32, (1, LANES), 1)
    total = hidden[0]
    prob_grad = jnp.zeros(prob.shape, f32)
    for expert in range(experts):
        column = jnp.where(
            choice[0, :, 0:1] == expert,
            slot[0, :, 0:1],
            jnp.where(choice[0, :, 1:2] == expert, slot[0, :, 1:2], -1),
        )
        rows = dot_nn(one_hot(column, places), returned[expert])
        total = total + prob[:, expert : expert + 1] * rows
        prob_grad = prob_grad + jnp.where(
            lane == expert, jnp.sum(up * rows, axis=-1, keepdims=True), 0.0
        )
    out_o[0] = total[0:patches, :].astype(bf16)
    inner = jnp.sum(prob * prob_grad, axis=-1, keepdims=True)
    logit = (prob * (prob_grad - inner)).astype(bf16)
    logit_o[0] = logit

    @pl.when(pl.program_id(0) == 0)
    def _():
        router_o[...] = jnp.zeros(router_o.shape, f32)

    router_o[...] += dot_tn(logit, routed[0])


def combine(choice, slot, returned, hidden, upstream, probs, routed, patches, after, later):
    count, padded, width = hidden.shape
    return pl.pallas_call(
        functools.partial(combine_body, patches=patches),
        grid=(count,),
        in_specs=[
            per((padded, 2)),
            per((padded, 2)),
            full(returned.shape),
            per((padded, width)),
            per((padded, width)),
            per((padded, LANES)),
            per((padded, width)),
            pl.BlockSpec(memory_space=pl.ANY),
            pl.BlockSpec(memory_space=pl.ANY),
        ],
        out_specs=[per((patches, width)), per((padded, LANES)), full((LANES, width))],
        out_shape=[
            jax.ShapeDtypeStruct((count, patches, width), bf16),
            jax.ShapeDtypeStruct((count, padded, LANES), bf16),
            jax.ShapeDtypeStruct((LANES, width), f32),
        ],
        compiler_params=params(),
        name="combine",
    )(choice, slot, returned, hidden, upstream, probs, routed, after, later)


def back_body(
    owner, choice, slot, returned, logit, router_w, hidden, upstream, gains, out_w, mixed, qkv, attn, qkv_w, img,
    grad_o, tile_o, gain_o,
    rows, normed_all, qkv_grad_all, mixed_all, branch_all, mixed_grad_s, hidden_grad_s,
    normed_turned, mixed_turned,
    *, patches, places
):
    image = pl.program_id(0)
    padded, width = rows.shape
    base = pl.multiple_of(image * padded, 16)
    here = pl.ds(base, padded)
    place = jnp.where(slot[0] >= 0, choice[0] * places + slot[0], -1)
    grid_places = lax.broadcasted_iota(jnp.int32, (padded, returned.shape[0]), 1)
    hits = (place[:, 0:1] == grid_places) | (place[:, 1:2] == grid_places)
    table = jnp.where(hits, 1.0, 0.0).astype(bf16)
    routed_grad = dot_nt(logit[0], router_w[...]) + dot_nn(table, returned[...])
    unit_two, inv_two = norm_stats(hidden[0])
    norm_grad, gain_two = norm_back(routed_grad, unit_two, inv_two, gains[1:2, :])
    hidden_grad = upstream[0].astype(f32) + norm_grad
    hidden_grad_s[...] = hidden_grad
    branch = hidden_grad.astype(bf16)
    branch_all[here, :] = branch
    mixed_all[here, :] = mixed[0]
    mixed_grad_s[...] = dot_nt(branch, out_w[...]).astype(bf16)
    low_half = lax.broadcasted_iota(jnp.int32, (1, LANES), 1) < HEAD_DIM
    halves = (low_half.astype(f32).astype(bf16), (1.0 - low_half.astype(f32)).astype(bf16))
    for pair in range(PAIRS):
        cols = slice(pair * LANES, (pair + 1) * LANES)
        q = qkv[0, :, pair * LANES : (pair + 1) * LANES]
        k = qkv[0, :, width + pair * LANES : width + (pair + 1) * LANES]
        v = qkv[0, :, 2 * width + pair * LANES : 2 * width + (pair + 1) * LANES]
        mg = mixed_grad_s[:, cols]
        q_grads, k_grads, v_grads = [], [], []
        for half in range(2):
            low = attn[0, 2 * pair + half]
            weights = low.astype(f32)
            weight_grad = dot_nt(mg * halves[half], v)
            product = weights * weight_grad
            inner = jnp.sum(product, axis=-1, keepdims=True)
            score = (product - weights * inner).astype(bf16)
            q_grads.append(dot_nn(score, k))
            k_grads.append(dot_tn(score, q))
            v_grads.append(dot_tn(low, mg))
        qkv_grad_all[here, pair * LANES : (pair + 1) * LANES] = (
            jnp.where(low_half, q_grads[0], q_grads[1]) * score_scale
        ).astype(bf16)
        qkv_grad_all[here, width + pair * LANES : width + (pair + 1) * LANES] = (
            jnp.where(low_half, k_grads[0], k_grads[1]) * score_scale
        ).astype(bf16)
        qkv_grad_all[here, 2 * width + pair * LANES : 2 * width + (pair + 1) * LANES] = jnp.where(
            low_half, v_grads[0], v_grads[1]
        ).astype(bf16)
    rows[...] = jnp.zeros(rows.shape, f32)
    rows[0:patches, :] = img[0].astype(f32)
    unit_one, inv_one = norm_stats(rows[...])
    normed_all[here, :] = (unit_one * gains[0:1, :]).astype(bf16)
    normed_grad = dot_nt(qkv_grad_all[here, :], qkv_w[...])
    norm_grad_one, gain_one = norm_back(normed_grad, unit_one, inv_one, gains[0:1, :])
    grad_o[0] = (hidden_grad_s[...] + norm_grad_one)[0:patches, :]

    @pl.when(image == 0)
    def _():
        gain_o[...] = jnp.zeros(gain_o.shape, f32)

    gain_o[0:1, :] += gain_one
    gain_o[1:2, :] += gain_two

    @pl.when(image == pl.num_programs(0) - 1)
    def _():
        normed_turned[...] = turn(normed_all[...])
        mixed_turned[...] = turn(mixed_all[...])
        row_tiles = width // TILE
        qkv_cols = 3 * row_tiles
        qkv_count = row_tiles * qkv_cols

        def one(s, carry):
            tile = owner[s]

            @pl.when(tile < qkv_count)
            def _():
                row = pl.multiple_of(tile // qkv_cols * TILE, TILE)
                col = pl.multiple_of(tile % qkv_cols * TILE, TILE)
                tile_o[s] = dot_nn(
                    normed_turned[pl.ds(row, TILE), :], qkv_grad_all[:, pl.ds(col, TILE)]
                ).astype(bf16)

            @pl.when(tile >= qkv_count)
            def _():
                rest = tile - qkv_count
                row = pl.multiple_of(rest // row_tiles * TILE, TILE)
                col = pl.multiple_of(rest % row_tiles * TILE, TILE)
                tile_o[s] = dot_nn(
                    mixed_turned[pl.ds(row, TILE), :], branch_all[:, pl.ds(col, TILE)]
                ).astype(bf16)

            return carry

        lax.fori_loop(0, tile_o.shape[0], one, 0)


def back(owner, choice, slot, returned, logit, router_pad, hidden, upstream, gains, out_w, mixed, qkv, attn, qkv_w,
         images, places):
    count, patches, width = images.shape
    padded = hidden.shape[1]
    tiles = owner.shape[0]
    return pl.pallas_call(
        functools.partial(back_body, patches=patches, places=places),
        grid_spec=pltpu.PrefetchScalarGridSpec(
            num_scalar_prefetch=1,
            grid=(count,),
            in_specs=[
                per((padded, 2)),
                per((padded, 2)),
                full(returned.shape),
                per((padded, LANES)),
                full(router_pad.shape),
                per((padded, width)),
                per((padded, width)),
                full(gains.shape),
                full(out_w.shape),
                per((padded, width)),
                per((padded, 3 * width)),
                per((HEADS, padded, padded)),
                full(qkv_w.shape),
                per((patches, width)),
            ],
            out_specs=[per((patches, width)), full((tiles, TILE, TILE)), full((8, width))],
            scratch_shapes=[
                pltpu.VMEM((padded, width), f32),
                pltpu.VMEM((count * padded, width), bf16),
                pltpu.VMEM((count * padded, 3 * width), bf16),
                pltpu.VMEM((count * padded, width), bf16),
                pltpu.VMEM((count * padded, width), bf16),
                pltpu.VMEM((padded, width), bf16),
                pltpu.VMEM((padded, width), f32),
                pltpu.VMEM((width, count * padded), bf16),
                pltpu.VMEM((width, count * padded), bf16),
            ],
        ),
        out_shape=[
            jax.ShapeDtypeStruct((count, patches, width), f32),
            jax.ShapeDtypeStruct((tiles, TILE, TILE), bf16),
            jax.ShapeDtypeStruct((8, width), f32),
        ],
        compiler_params=params(),
        name="back",
    )(owner, choice, slot, returned, logit, router_pad, hidden, upstream, gains, out_w, mixed, qkv, attn, qkv_w, images)


def adam_body(owner, grad, w_one, w_two, m, v, left, right, m_o, v_o, w_o, low_o, *, first_count):
    tile = owner[pl.program_id(0)]
    first = (tile < first_count).astype(f32)
    old = w_one[...].astype(f32) * first + w_two[...].astype(f32) * (1.0 - first)
    left_low = left[0].astype(bf16)
    right_low = right[0].astype(bf16)
    turned = dot_nn(dot_tn(left_low, grad[0].astype(bf16)).astype(bf16), right_low)
    m_new = adam_beta * m[0] + (1.0 - adam_beta) * turned
    v_new = adam_beta * v[0] + (1.0 - adam_beta) * turned * turned
    m_o[0] = m_new
    v_o[0] = v_new
    direction = m_new / correction / (jnp.sqrt(v_new / correction) + adam_eps)
    back_turn = dot_nt(dot_nn(left_low, direction.astype(bf16)).astype(bf16), right_low)
    rate = rate_scale * jnp.sqrt(jnp.mean(old * old))
    new = old - rate * back_turn
    w_o[0] = new
    low_o[0] = new.astype(bf16)


def rotated_adam(owner, grad, w_one, w_two, m, v, left, right):
    count = m.shape[0]
    one_cols = w_one.shape[1] // TILE
    two_cols = w_two.shape[1] // TILE
    first_count = w_one.shape[0] // TILE * one_cols

    def one_at(i, owner):
        tile = jnp.minimum(owner[i], first_count - 1)
        return (tile // one_cols, tile % one_cols)

    def two_at(i, owner):
        tile = jnp.maximum(owner[i] - first_count, 0)
        return (tile // two_cols, tile % two_cols)

    spec = per((TILE, TILE))
    shape = jax.ShapeDtypeStruct((count, TILE, TILE), f32)
    return pl.pallas_call(
        functools.partial(adam_body, first_count=first_count),
        grid_spec=pltpu.PrefetchScalarGridSpec(
            num_scalar_prefetch=1,
            grid=(count,),
            in_specs=[
                spec,
                pl.BlockSpec((TILE, TILE), one_at),
                pl.BlockSpec((TILE, TILE), two_at),
                spec,
                spec,
                spec,
                spec,
            ],
            out_specs=[spec, spec, spec, spec],
        ),
        out_shape=[shape, shape, shape, jax.ShapeDtypeStruct((count, TILE, TILE), bf16)],
        compiler_params=params(),
        name="adam",
    )(owner, grad, w_one, w_two, m, v, left, right)


def untile_body(slot_of, *refs):
    outs = refs[-2:]
    tiles = refs[:-2]
    for out in outs:
        cols = out.shape[1] // TILE
        count = out.shape[0] // TILE * cols
        for index in range(count):
            row, col = index // cols * TILE, index % cols * TILE
            out[row : row + TILE, col : col + TILE] = tiles[index][0]
        tiles = tiles[count:]


def untile(slot_of, tiles, one_shape, two_shape, one_blocks, two_blocks):
    steps = one_blocks
    specs = []
    one_rows, one_cols = one_shape[0] // TILE, one_shape[1] // TILE
    two_rows, two_cols = two_shape[0] // TILE, two_shape[1] // TILE
    wide = one_cols // steps
    high = two_rows // two_blocks
    for row in range(one_rows):
        for col in range(wide):
            specs.append(
                pl.BlockSpec(
                    (1, TILE, TILE),
                    lambda i, slot_of, row=row, col=col: (slot_of[row * one_cols + i * wide + col], 0, 0),
                )
            )
    base = one_rows * one_cols
    for row in range(high):
        for col in range(two_cols):
            specs.append(
                pl.BlockSpec(
                    (1, TILE, TILE),
                    lambda i, slot_of, row=row, col=col: (
                        slot_of[base + (jnp.minimum(i, two_blocks - 1) * high + row) * two_cols + col], 0, 0,
                    ),
                )
            )
    return pl.pallas_call(
        untile_body,
        grid_spec=pltpu.PrefetchScalarGridSpec(
            num_scalar_prefetch=1,
            grid=(steps,),
            in_specs=specs,
            out_specs=[
                pl.BlockSpec((one_shape[0], wide * TILE), lambda i, slot_of: (0, i)),
                pl.BlockSpec(
                    (high * TILE, two_shape[1]),
                    lambda i, slot_of: (jnp.minimum(i, two_blocks - 1), 0),
                ),
            ],
        ),
        out_shape=[jax.ShapeDtypeStruct(one_shape, bf16), jax.ShapeDtypeStruct(two_shape, bf16)],
        compiler_params=params(),
        name="untile",
    )(slot_of, *([tiles] * len(specs)))


def inverse(owner):
    ids = jnp.arange(owner.shape[0], dtype=jnp.int32)
    return jnp.sum(jnp.where(owner[None, :] == ids[:, None], ids[None, :], 0), axis=1)


def sum_over_expert(rows):
    size = lax.axis_size("expert")
    bits = [1 << b for b in range(size.bit_length() - 1)]
    half = rows.shape[1] // 2
    parts = [rows[:, :half], rows[:, half:]]
    for step in range(len(bits)):
        for which in range(2):
            bit = bits[step] if which == 0 else bits[-1 - step]
            other = lax.ppermute(parts[which], "expert", [(i, i ^ bit) for i in range(size)])
            parts[which] = (parts[which].astype(f32) + other.astype(f32)).astype(bf16)
    return jnp.concatenate(parts, axis=1)


def plain_adam(grad_values, weight_values, first_moment, second_moment, axes):
    first_new = adam_beta * first_moment + (1.0 - adam_beta) * grad_values
    second_new = adam_beta * second_moment + (1.0 - adam_beta) * grad_values * grad_values
    direction = first_new / correction / (jnp.sqrt(second_new / correction) + adam_eps)
    step_rate = rate_scale * jnp.sqrt(
        jnp.mean(weight_values * weight_values, axis=axes, keepdims=True)
    )
    return (first_new, second_new, weight_values - step_rate * direction)


def step(
    images,
    cotangent,
    gains,
    qkv_weight,
    out_weight,
    router_weight,
    up_weight,
    down_weight,
    choices,
    slots,
    owner_shared,
    owner_expert,
    shared_m,
    shared_v,
    shared_left,
    shared_right,
    expert_m,
    expert_v,
    expert_left,
    expert_right,
    router_m,
    router_v,
    gains_m,
    gains_v,
):
    count, patches, width = images.shape
    hidden_width = up_weight.shape[2]
    experts = router_weight.shape[1]
    dp_size = lax.axis_size("dp")
    dp_index = lax.axis_index("dp")
    capacity = (42 * count * patches + 20 * experts - 1) // (20 * experts)
    places = round_up(capacity, 16)
    padded = round_up(patches, 16)
    tokens = count * padded
    router_pad = jnp.pad(router_weight, ((0, 0), (0, LANES - experts)))
    spare = ((0, 0), (0, padded - patches), (0, 0))
    choice = jnp.pad(choices, spare)
    slot = jnp.pad(slots, spare, constant_values=-1)
    choice_rows = choice.reshape(tokens, 2).T
    slot_rows = slot.reshape(tokens, 2).T

    qkv, attn, mixed, hidden, routed, probs, upstream = front(
        images, cotangent, gains, qkv_weight, out_weight, router_pad, experts, padded
    )
    outgoing, outgoing_grad = dispatch(
        choice_rows,
        slot_rows,
        routed.reshape(tokens, width),
        probs.reshape(tokens, LANES),
        upstream.reshape(tokens, width),
        experts,
        places,
    )

    def exchange(rows):
        return lax.all_to_all(rows, "expert", split_axis=0, concat_axis=0, tiled=True)

    total_places = experts * places
    arriving = exchange(outgoing).reshape(total_places, width)
    arriving_grad = exchange(outgoing_grad).reshape(total_places, width)
    act, slope, produced = ffn_fwd(arriving, up_weight, down_weight)
    returned = exchange(produced.reshape(experts, places, width))
    pre_grad, in_grad = ffn_bwd(arriving_grad, slope, up_weight, down_weight)
    returned_grad = exchange(in_grad.reshape(experts, places, width)).reshape(total_places, width)
    owner_row = owner_expert[0]
    expert_slot = inverse(owner_row)
    shared_slot = inverse(owner_shared)
    expert_grads = expert_dw(expert_slot, arriving, arriving_grad, act, pre_grad, returned)
    expert_own = lax.psum_scatter(expert_grads, "dp", scatter_dimension=0, tiled=True)
    out, logit_low, router_grad = combine(
        choice, slot, returned, hidden, upstream, probs, routed, patches, expert_grads, expert_grads
    )
    grad_input, shared_grads, gain_grads = back(
        owner_shared, choice, slot, returned_grad, logit_low, router_pad, hidden, upstream, gains, out_weight,
        mixed, qkv, attn, qkv_weight, images, places,
    )
    shared_grads, expert_own = lax.optimization_barrier((shared_grads, expert_own))
    shared_part = lax.psum_scatter(shared_grads, "dp", scatter_dimension=0, tiled=True)
    shared_own = sum_over_expert(shared_part)
    small = lax.psum(
        jnp.concatenate([router_grad[: round_up(experts, 8)], gain_grads], axis=0), ("dp", "expert")
    )
    router_total = small[:experts].T
    gains_total = small[round_up(experts, 8) : round_up(experts, 8) + 2]

    own_shared = owner_shared.shape[0] // dp_size
    own_expert = owner_row.shape[0] // dp_size
    my_shared = lax.dynamic_slice_in_dim(owner_shared, dp_index * own_shared, own_shared)
    my_expert = lax.dynamic_slice_in_dim(owner_row, dp_index * own_expert, own_expert)
    expert_m_new, expert_v_new, expert_w_new, expert_low = rotated_adam(
        my_expert, expert_own, up_weight[0], down_weight[0],
        expert_m[0], expert_v[0], expert_left[0], expert_right[0],
    )
    expert_all = lax.all_gather(expert_low, "dp", axis=0, tiled=True)
    shared_m_new, shared_v_new, shared_w_new, shared_low = rotated_adam(
        my_shared, shared_own, qkv_weight, out_weight, shared_m, shared_v, shared_left, shared_right
    )
    shared_all = lax.all_gather(shared_low, "dp", axis=0, tiled=True)
    router_m_new, router_v_new, router_w_new = plain_adam(
        router_total, router_weight.astype(f32), router_m, router_v, (0, 1)
    )
    gains_m_new, gains_v_new, gains_w_new = plain_adam(gains_total, gains, gains_m, gains_v, (1,))

    up_copy, down_copy = untile(
        expert_slot, expert_all, (width, hidden_width), (hidden_width, width), 4, 4
    )
    qkv_copy, out_copy = untile(shared_slot, shared_all, (width, 3 * width), (width, width), 3, 2)
    return (
        out,
        grad_input,
        shared_m_new,
        shared_v_new,
        shared_w_new,
        expert_m_new[None],
        expert_v_new[None],
        expert_w_new[None],
        router_m_new,
        router_v_new,
        router_w_new,
        gains_m_new,
        gains_v_new,
        gains_w_new,
        qkv_copy,
        out_copy,
        up_copy[None],
        down_copy[None],
    )


def solution(mesh):
    rows = P(("dp", "expert"), None, None)
    shared = P("dp", None, None)
    expert = P("expert", "dp", None, None)
    weight = P("expert", None, None)
    return jax.shard_map(
        step,
        mesh=mesh,
        in_specs=(
            (rows, rows) + (P(),) * 4 + (weight, weight, rows, rows, P(), P("expert", None))
            + (shared,) * 4 + (expert,) * 4 + (P(),) * 4
        ),
        out_specs=(
            (rows, rows) + (shared,) * 3 + (expert,) * 3 + (P(),) * 8 + (weight, weight)
        ),
        check_vma=False,
    )
```
